128 devices in a mesh: samp: 8 (over z, y_hi), feat: 16 (over y_lo, x, core).
Axes of the slice: x: 4, y: 4 (y_hi: 2, y_lo: 2; y = y_hi * 2 + y_lo), z: 4, core: 2. Of those that a mesh axis runs over, the one named last changes fastest.
Arguments:
- inputs: bfloat16 [440, 32768], P(None, ('samp', 'feat')), may hold values from -6 to 6
- probs: bfloat16 [147, 32768], P(None, ('samp', 'feat')), may hold values from 0 to 1, as said below
- labels: int32 [32768], P(('samp', 'feat')), may hold values from 0 to 146
- proj_weight: bfloat16 [440, 32768], P(None, ('feat', 'samp')), may hold values from -0.25 to 0.25
- phase: bfloat16 [1, 32768], P(None, ('feat', 'samp')), may hold values from -3.140625 to 3.140625
- direction: bfloat16 [147, 32768], P(None, ('feat', 'samp')), may hold values from -0.03125 to 0.03125
- damping: float32 [1], replicated, may hold values from 300 to 3000
Outputs:
- hess_vec: float32 [147, 32768], P(None, ('feat', 'samp'))
- gradient: float32 [147, 32768], P(None, ('feat', 'samp'))
The draws below stay inside these ranges and needn't reach their ends.
Inputs may be any that keep to these rules, and one draw needn't show every extreme that they name: Each column of probs is positive and sums to one up to rounding.
All inputs are finite; a program needn't handle non-finite values.
Results may differ from the reference program's by a relative error of at most 0.005.
The reference program's roundings to bfloat16 on the way count: a program that leaves them out, or rounds other values in their place, can miss the bound.
Values may be sent and summed in bfloat16 or wider, within the bound.
A program may use at most 64 MiB of HBM per device.

```python
import math
import jax
import jax.numpy as jnp
from jax import lax

RAW = 440
C = 147
F = 32768
SAMPLES = 32768


def draw_probs(key, part):
    key_top = jax.random.fold_in(key, 11)
    key_rest = jax.random.fold_in(key, 23)
    key_lift = jax.random.fold_in(key, 37)
    chosen = jax.random.randint(key_top, (1, SAMPLES), 0, C)
    class_ids = lax.broadcasted_iota(jnp.int32, (C, SAMPLES), 0)
    marked = (class_ids == chosen).astype(jnp.float32)
    base_lift = math.log(C - 1.0)
    rest = 0.3 * jax.random.normal(key_rest, (C, SAMPLES), jnp.float32)
    lift = base_lift + 1.0 + 0.0 * jax.random.uniform(key_lift, (1, SAMPLES), jnp.float32)
    logits = rest + lift * marked
    return jax.nn.softmax(logits, axis=0).astype(jnp.bfloat16)


def set_ends(values, key, least, largest):
    longest = values.shape.index(max(values.shape))
    spots = []
    for shift in (0, 1):
        where = [jax.random.randint(jax.random.fold_in(key, axis), (), 0, length) for axis, length in enumerate(values.shape)]
        where[longest] = (where[longest] + shift) % values.shape[longest]
        spots.append(tuple(where))
    return values.at[spots[0]].set(least).at[spots[1]].set(largest)


def levels(own_key, extent, shards, low, top_value):
    def one(axis_at, shards_of):
        steps = jax.random.uniform(jax.random.fold_in(jax.random.fold_in(own_key, 6), axis_at), (shards_of,), jnp.float32, low / len(shards), top_value / len(shards))
        return jnp.repeat(jnp.exp(steps), extent[axis_at] // shards_of).reshape((-1,) + (1,) * (len(extent) - axis_at - 1))

    level = one(*shards[0])
    for cut in shards[1:]:
        level = level * one(*cut)
    return level


def gaussian(own_key, extent, scale, limit, shards=(), held_as=jnp.bfloat16):
    result = scale * jax.random.normal(own_key, extent, jnp.float32)
    if shards:
        result = result * levels(own_key, extent, shards, -0.22, 0.18)
    return jnp.clip(result, -limit, limit).astype(held_as)


def setup_inputs(seed: int = 0) -> dict:
    key_of = jax.random.split(jax.random.key(seed), 8)
    inputs = gaussian(key_of[0], (RAW, SAMPLES), 1.0, 6.0, ((1, 128),))
    probs = draw_probs(jax.random.fold_in(key_of[7], 71), 0)
    labels = set_ends(jax.random.randint(key_of[2], (SAMPLES,), 0, C), jax.random.fold_in(key_of[2], 1), 0, C - 1).astype(jnp.int32)
    proj_weight = gaussian(key_of[3], (RAW, F), RAW ** -0.5, 0.25, ((1, 128),))
    phase = jnp.clip(jax.random.uniform(key_of[4], (1, F), jnp.float32, -3.140625, 3.140625), -3.140625, 3.140625).astype(jnp.bfloat16)
    direction = gaussian(key_of[5], (C, F), F ** -0.5, 0.03125, ((1, 128),))
    damping = jnp.clip(jnp.exp(jax.random.uniform(key_of[6], (1,), jnp.float32, math.log(300.0), math.log(3000.0))), 300.0, 3000.0)
    return {"inputs": inputs, "probs": probs, "labels": labels, "proj_weight": proj_weight, "phase": phase, "direction": direction, "damping": damping}


def reference(inputs, probs, labels, proj_weight, phase, direction, damping):
    block = min(1024, SAMPLES)
    count = SAMPLES // block
    x_blocks = inputs.reshape(RAW, count, block).transpose(1, 0, 2)
    p_blocks = probs.reshape(C, count, block).transpose(1, 0, 2)
    l_blocks = labels.reshape(count, block)
    phase_col = phase.astype(jnp.float32).T
    classes = lax.broadcasted_iota(jnp.int32, (C, block), 0)

    def step(carry, pieces):
        hv_acc, grad_acc = carry
        x_block, p_block, l_block = pieces
        proj = lax.dot_general(proj_weight, x_block, (((0,), (0,)), ((), ())), preferred_element_type=jnp.float32)
        feats = jnp.cos(proj + phase_col).astype(jnp.bfloat16)
        tangent = jnp.dot(direction, feats, preferred_element_type=jnp.float32)
        prob = p_block.astype(jnp.float32)
        mixed = jnp.sum(prob * tangent, axis=0, keepdims=True)
        curv = (prob * (tangent - mixed)).astype(jnp.bfloat16)
        onehot = (classes == l_block[None, :]).astype(jnp.float32)
        resid = (prob - onehot).astype(jnp.bfloat16)
        dims = (((1,), (1,)), ((), ()))
        hv_acc = hv_acc + lax.dot_general(curv, feats, dims, preferred_element_type=jnp.float32)
        grad_acc = grad_acc + lax.dot_general(resid, feats, dims, preferred_element_type=jnp.float32)
        return (hv_acc, grad_acc), None

    start = (jnp.zeros((C, F), jnp.float32), jnp.zeros((C, F), jnp.float32))
    (hv_acc, grad_acc), _ = lax.scan(step, start, (x_blocks, p_blocks, l_blocks))
    hess_vec = hv_acc + damping[0] * direction.astype(jnp.float32)
    return hess_vec, grad_acc
```

```python
import math

import jax
import jax.numpy as jnp
from jax import lax
from jax.experimental import pallas as pl
from jax.experimental.pallas import tpu as pltpu
from jax.sharding import PartitionSpec as P

MESH = pl.DeviceIdType.MESH
BF = jnp.bfloat16
F32 = jnp.float32
TURN = 1.0 / (2.0 * math.pi)
SINE = (6.283185160088606, -41.34165503119389, 81.60100405839074, -76.54978193238271, 39.536703184435794)

RAWP = 448
CP = 160
WROWS = RAWP + CP
KX = 512

XQ = ((0, 0), (3, 0), (1, 0), (0, 1), (2, 0), (3, 1), (1, 1), (2, 1))
WQ = ((0, 0), (3, 0), (1, 0), (0, 1), (2, 0), (3, 1), (1, 1), (2, 1))
XS = tuple((dx, dy, dc) for dx, dy in XQ for dc in (0, 1))


def xslot(dx, dy, dc):
    return XS.index((dx % 4, dy % 2, dc % 2))


def wslot(dz, dy):
    return WQ.index((dz % 4, dy % 2))


def cosine(u):
    t = u * TURN
    y = 0.25 - jnp.abs(t - jnp.round(t))
    z = y * y
    p = F32(SINE[-1])
    for c in SINE[-2::-1]:
        p = p * z + F32(c)
    return (p * y).astype(BF)


def kernel(x_ref, prob_ref, lab_ref, w_ref, ph_ref, dir_ref, damp_ref, hess_ref, grad_ref,
           xg, wg, feats, dirb, tsend, trecv, resid, curv, gsend, grecv, hsend, hrecv,
           loc_sem, xs_sem, xr_sem, ws_sem, wr_sem, ts_sem, tr_sem, rs_sem, rr_sem,
           cs_sem, cr_sem, gs_sem, gr_sem, hs_sem, hr_sem):
    samp = lax.axis_index("samp")
    feat = lax.axis_index("feat")
    z, yh = samp // 2, samp % 2
    yl, x, core = feat // 8, (feat // 2) % 4, feat % 2

    def dev(dx=0, dyl=0, dc=0, dz=0, dyh=0):
        s = ((z + dz) % 4) * 2 + (yh + dyh) % 2
        f = (((yl + dyl) % 2) * 4 + (x + dx) % 4) * 2 + (core + dc) % 2
        return (s, f)

    barrier = pltpu.get_barrier_semaphore()
    for dx, dy, dc in XS[1:]:
        pl.semaphore_signal(barrier, inc=1, device_id=dev(dx=dx, dyl=dy, dc=dc), device_id_type=MESH)
    for dz, dy in WQ[1:]:
        pl.semaphore_signal(barrier, inc=1, device_id=dev(dz=dz, dyh=dy), device_id_type=MESH)

    wv = jnp.concatenate(
        [w_ref[...].astype(F32),
         jnp.where(lax.broadcasted_iota(jnp.int32, (8, 256), 0) == 0, ph_ref[...].astype(F32), 0.0)], axis=0)
    wg[0, 0:RAWP, :] = wv.astype(BF)
    wg[0, WROWS - 16:WROWS, :] = jnp.zeros((16, 256), BF)
    wg[0, RAWP:RAWP + 147, :] = dir_ref[...]
    xv = jnp.concatenate(
        [x_ref[...].astype(F32),
         jnp.where(lax.broadcasted_iota(jnp.int32, (KX - 440, 256), 0) == 0, 1.0, 0.0)], axis=0)
    xg[0] = xv.T.astype(BF)
    prob = prob_ref[...].astype(F32)
    onehot = (lax.broadcasted_iota(jnp.int32, (147, 256), 0) == lab_ref[...]).astype(F32)
    resid[CP - 16:CP, 0:256] = jnp.zeros((16, 256), BF)
    resid[0:147, 0:256] = (prob - onehot).astype(BF)

    pl.semaphore_wait(barrier, 22)

    sends = []

    def put(src, dst, ssem, rsem, target):
        c = pltpu.make_async_remote_copy(
            src_ref=src, dst_ref=dst, send_sem=ssem, recv_sem=rsem, device_id=target, device_id_type=MESH)
        c.start()
        sends.append(c)

    nx = [0]
    nw = [0]

    def xput(frm, to, target, half=None):
        k = nx[0]
        nx[0] += 1
        if half is None:
            put(xg.at[frm], xg.at[to], xs_sem.at[k], xr_sem.at[to, 0], target)
        else:
            rows = pl.ds(half * 128, 128)
            put(xg.at[frm, rows], xg.at[to, rows], xs_sem.at[k], xr_sem.at[to, half], target)

    def wput(frm, to, target, half=None):
        k = nw[0]
        nw[0] += 1
        if half is None:
            put(wg.at[frm], wg.at[to], ws_sem.at[k], wr_sem.at[to, 0], target)
        else:
            rows = pl.ds(half * (WROWS // 2), WROWS // 2)
            put(wg.at[frm, rows], wg.at[to, rows], ws_sem.at[k], wr_sem.at[to, half], target)

    def wait_in(ref, sem):
        pltpu.make_async_copy(ref, ref, sem).wait()

    def xwait(k):
        dx, dy, dc = XS[k]
        if dx == 2 and dc == 0:
            for h in (0, 1):
                rows = pl.ds(h * 128, 128)
                wait_in(xg.at[k, rows], xr_sem.at[k, h])
        else:
            wait_in(xg.at[k], xr_sem.at[k, 0])

    def wwait(k):
        dz, dy = WQ[k]
        if dz == 2:
            for h in (0, 1):
                rows = pl.ds(h * (WROWS // 2), WROWS // 2)
                wait_in(wg.at[k, rows], wr_sem.at[k, h])
        else:
            wait_in(wg.at[k], wr_sem.at[k, 0])

    xp, xm = dev(dx=1), dev(dx=3)
    zp, zm = dev(dz=1), dev(dz=3)
    sib = dev(dc=1)

    wput(0, wslot(3, 0), zp)
    wput(0, wslot(1, 0), zm)
    wput(0, wslot(0, 1), dev(dyh=1))
    xput(0, xslot(3, 0, 0), xp)
    xput(0, xslot(1, 0, 0), xm)
    xput(0, xslot(0, 1, 0), dev(dyl=1))
    xput(0, xslot(0, 0, 1), sib)

    def wfwd(k):
        wwait(k)
        dz, dy = WQ[k]
        if dz == 0:
            wput(k, wslot(3, dy), zp)
            wput(k, wslot(1, dy), zm)
        elif dz == 3:
            wput(k, wslot(2, dy), zp, 0)
        elif dz == 1:
            wput(k, wslot(2, dy), zm, 1)

    def xfwd(k):
        xwait(k)
        dx, dy, dc = XS[k]
        if dx == 0:
            xput(k, xslot(3, dy, 0), xp)
            xput(k, xslot(1, dy, 0), xm)
        elif dx == 3:
            xput(k, xslot(2, dy, 0), xp, 0)
        elif dx == 1:
            xput(k, xslot(2, dy, 0), xm, 1)
        xput(k, xslot(dx, dy, 1), sib)

    for q in range(1, 8):
        wfwd(q)
        xfwd(2 * q)

    for j in range(8):
        dirb[:, j * 256:(j + 1) * 256] = wg[j, RAWP:WROWS, :]
    for q in range(8):
        xwait(2 * q + 1)

    def spread(buf, s_sem, r_sem):
        for i, (dx, dy) in enumerate(XQ[1:]):
            to = xslot(-dx, dy, 0)
            put(buf.at[:, pl.ds(0, 256)], buf.at[:, pl.ds(to * 256, 256)],
                s_sem.at[i], r_sem.at[to], dev(dx=dx, dyl=dy))
        to = xslot(0, 0, 1)
        put(buf.at[:, pl.ds(0, 256)], buf.at[:, pl.ds(to * 256, 256)], s_sem.at[7], r_sem.at[to], sib)

    def relay(buf, s_sem, r_sem):
        for i, (dx, dy) in enumerate(XQ[1:]):
            k, to = xslot(dx, dy, 0), xslot(dx, dy, 1)
            wait_in(buf.at[:, pl.ds(k * 256, 256)], r_sem.at[k])
            put(buf.at[:, pl.ds(k * 256, 256)], buf.at[:, pl.ds(to * 256, 256)],
                s_sem.at[8 + i], r_sem.at[to], sib)
        for dx, dy in XQ:
            k = xslot(dx, dy, 1)
            wait_in(buf.at[:, pl.ds(k * 256, 256)], r_sem.at[k])

    spread(resid, rs_sem, rr_sem)

    def tcopy(k):
        dx, dy, dc = XS[k]
        to = xslot(-dx, dy, dc)
        return pltpu.make_async_remote_copy(
            src_ref=tsend.at[k], dst_ref=trecv.at[to], send_sem=ts_sem.at[k], recv_sem=tr_sem.at[to],
            device_id=dev(dx=dx, dyl=dy, dc=dc), device_id_type=MESH)

    def shard(step, carry):
        i = 15 - step
        rows = pl.ds(pl.multiple_of(i * 256, 256), 256)
        xv = xg[i]
        for j in range(8):
            u = jnp.dot(xv, wg[j, 0:KX, :], preferred_element_type=F32)
            feats[rows, j * 256:(j + 1) * 256] = cosine(u)
        t = lax.dot_general(feats[rows, :], dirb[...], (((1,), (1,)), ((), ())), preferred_element_type=F32)
        tsend[i] = t.T.astype(BF)
        for k in range(1, 16):
            @pl.when(i == k)
            def _():
                tcopy(k).start()
        return carry

    lax.fori_loop(0, 16, shard, 0)
    relay(resid, rs_sem, rr_sem)

    total = tsend[0].astype(F32)
    for k in range(1, 16):
        wait_in(trecv.at[k], tr_sem.at[k])
        total = total + trecv[k].astype(F32)
    total = total[0:147]
    mixed = jnp.sum(prob * total, axis=0, keepdims=True)
    curv[CP - 16:CP, 0:256] = jnp.zeros((16, 256), BF)
    curv[0:147, 0:256] = (prob * (total - mixed)).astype(BF)
    spread(curv, cs_sem, cr_sem)

    def share(buf, own, send, recv, s_sem, r_sem):
        for j in (7, 5, 6, 4, 3, 1, 2, 0):
            v = jnp.dot(buf[...], feats[:, j * 256:(j + 1) * 256], preferred_element_type=F32)
            if j == 0:
                own[...] = v[0:147]
            else:
                dz, dy = WQ[j]
                to = wslot(-dz, dy)
                send[j] = v.astype(BF)
                put(send.at[j], recv.at[to], s_sem.at[j], r_sem.at[to], dev(dz=dz, dyh=dy))

    share(resid, grad_ref, gsend, grecv, gs_sem, gr_sem)
    relay(curv, cs_sem, cr_sem)
    share(curv, hess_ref, hsend, hrecv, hs_sem, hr_sem)

    g = grad_ref[...]
    for k in range(1, 8):
        wait_in(grecv.at[k], gr_sem.at[k])
        g = g + grecv[k].astype(F32)[0:147]
    grad_ref[...] = g
    h = hess_ref[...] + damp_ref[0] * dir_ref[...].astype(F32)
    for k in range(1, 8):
        wait_in(hrecv.at[k], hr_sem.at[k])
        h = h + hrecv[k].astype(F32)[0:147]
    hess_ref[...] = h

    for c in sends:
        c.wait_send()
    for k in range(1, 16):
        tcopy(k).wait_send()


def on_device(inputs, probs, labels, proj_weight, phase, direction, damping):
    vmem = pl.BlockSpec(memory_space=pltpu.VMEM)
    dma = pltpu.SemaphoreType.DMA
    out = jax.ShapeDtypeStruct(direction.shape, F32)
    return pl.pallas_call(
        kernel,
        out_shape=(out, out),
        in_specs=[vmem] * 6 + [pl.BlockSpec(memory_space=pltpu.SMEM)],
        out_specs=(vmem, vmem),
        scratch_shapes=[
            pltpu.VMEM((16, 256, KX), BF),
            pltpu.VMEM((8, WROWS, 256), BF),
            pltpu.VMEM((4096, 2048), BF),
            pltpu.VMEM((CP, 2048), BF),
            pltpu.VMEM((16, CP, 256), BF),
            pltpu.VMEM((16, CP, 256), BF),
            pltpu.VMEM((CP, 4096), BF),
            pltpu.VMEM((CP, 4096), BF),
            pltpu.VMEM((8, CP, 256), BF),
            pltpu.VMEM((8, CP, 256), BF),
            pltpu.VMEM((8, CP, 256), BF),
            pltpu.VMEM((8, CP, 256), BF),
            dma((1,)), dma((20,)), dma((16, 2)), dma((12,)), dma((8, 2)),
            dma((16,)), dma((16,)), dma((16,)), dma((16,)),
            dma((16,)), dma((16,)), dma((8,)), dma((8,)), dma((8,)), dma((8,)),
        ],
        compiler_params=pltpu.CompilerParams(
            collective_id=0, has_side_effects=True, vmem_limit_bytes=56 * 1024 * 1024),
    )(inputs, probs, labels.reshape(1, -1), proj_weight, phase, direction, damping)


def solution(mesh):
    placed = (
        P(None, ("samp", "feat")),
        P(None, ("samp", "feat")),
        P(("samp", "feat")),
        P(None, ("feat", "samp")),
        P(None, ("feat", "samp")),
        P(None, ("feat", "samp")),
        P(),
    )
    return jax.shard_map(
        on_device,
        mesh=mesh,
        in_specs=placed,
        out_specs=(P(None, ("feat", "samp")), P(None, ("feat", "samp"))),
        check_vma=False,
    )
```

```python
import math

import jax
import jax.numpy as jnp
from jax import lax
from jax.experimental import pallas as pl
from jax.experimental.pallas import tpu as pltpu
from jax.sharding import PartitionSpec as P

MESH = pl.DeviceIdType.MESH
BF = jnp.bfloat16
F32 = jnp.float32
TURN = 1.0 / (2.0 * math.pi)
SINE = (6.283185160088606, -41.34165503119389, 81.60100405839074, -76.54978193238271, 39.536703184435794)

RAWP = 448
CP = 160
KX = 512
HALF = 128
WH = RAWP // 2

RING = ((0, 0), (3, 0), (1, 0), (2, 0), (0, 1), (3, 1), (1, 1), (2, 1))


def chip(a, b):
    return RING.index((a % 4, b % 2))


def cosine(u):
    t = u * TURN
    y = 0.25 - jnp.abs(t - jnp.round(t))
    z = y * y
    p = F32(SINE[-1])
    for c in SINE[-2::-1]:
        p = p * z + F32(c)
    return (p * y).astype(BF)


def kernel(x_ref, prob_ref, lab_ref, w_ref, ph_ref, dir_ref, damp_ref, hess_ref, grad_ref,
           xg, wg, fa, fb, dirg, dirt, tkeep, tss, tsr, tse, trecv, resid, curv,
           gsend, grecv, hsend, hrecv, hacc, gkeep,
           xs_sem, xr_sem, ws_sem, wr_sem, ds_sem, dr_sem, bs_sem, br_sem, ts_sem, tr_sem,
           rs_sem, rr_sem, cs_sem, cr_sem, gs_sem, gr_sem, hs_sem, hr_sem):
    samp = lax.axis_index("samp")
    feat = lax.axis_index("feat")
    z, yh = samp // 2, samp % 2
    yl, x, core = feat // 8, (feat // 2) % 4, feat % 2

    def dev(dx=0, dyl=0, dc=0, dz=0, dyh=0):
        s = ((z + dz) % 4) * 2 + (yh + dyh) % 2
        f = (((yl + dyl) % 2) * 4 + (x + dx) % 4) * 2 + (core + dc) % 2
        return (s, f)

    xp, xm, x2, yp = dev(dx=1), dev(dx=3), dev(dx=2), dev(dyl=1)
    zp, zm, z2, yq = dev(dz=1), dev(dz=3), dev(dz=2), dev(dyh=1)
    sib = dev(dc=1)

    barrier = pltpu.get_barrier_semaphore()
    greet = [sib] + [dev(dx=a, dyl=b) for a, b in RING[1:]] + [dev(dz=a, dyh=b) for a, b in RING[1:]]
    for d in greet:
        pl.semaphore_signal(barrier, inc=1, device_id=d, device_id_type=MESH)

    wv = jnp.concatenate(
        [w_ref[...].astype(F32),
         jnp.where(lax.broadcasted_iota(jnp.int32, (8, 256), 0) == 0, ph_ref[...].astype(F32), 0.0)], axis=0)
    wg[0, 0:RAWP, :] = wv.astype(BF)
    for j in range(8):
        wg[j, RAWP:KX, :] = jnp.zeros((KX - RAWP, 256), BF)
    xv = jnp.concatenate(
        [x_ref[...].astype(F32),
         jnp.where(lax.broadcasted_iota(jnp.int32, (KX - 440, 256), 0) == 0, 1.0, 0.0)], axis=0)
    xt = xv.T.astype(BF)
    xg[0, 0] = xt[0:HALF]
    xg[1, 0] = xt[HALF:]
    dirg[0, CP - 16:CP, :] = jnp.zeros((16, 256), BF)
    dirg[0, 0:147, :] = dir_ref[...]
    prob = prob_ref[...].astype(F32)
    onehot = (lax.broadcasted_iota(jnp.int32, (147, 256), 0) == lab_ref[...]).astype(F32)
    own_resid = (prob - onehot).astype(BF)
    for p in (0, 1):
        lanes = slice(p * 2048, p * 2048 + HALF)
        resid[CP - 16:CP, lanes] = jnp.zeros((16, HALF), BF)
        resid[0:147, lanes] = own_resid[:, p * HALF:(p + 1) * HALF]
        curv[CP - 16:CP, lanes] = jnp.zeros((16, HALF), BF)

    pl.semaphore_wait(barrier, len(greet))

    sends = []
    used = {}

    def put(src, dst, ssems, rsem, target):
        k = used.get(id(ssems), 0)
        used[id(ssems)] = k + 1
        c = pltpu.make_async_remote_copy(
            src_ref=src, dst_ref=dst, send_sem=ssems.at[k], recv_sem=rsem, device_id=target, device_id_type=MESH)
        c.start()
        sends.append(c)

    def wait_in(ref, sem):
        pltpu.make_async_copy(ref, ref, sem).wait()

    def wput(frm, to, target, h):
        rows = pl.ds(h * WH, WH)
        put(wg.at[frm, rows], wg.at[to, rows], ws_sem, wr_sem.at[to, h], target)

    def wwait(k, h):
        wait_in(wg.at[k, pl.ds(h * WH, WH)], wr_sem.at[k, h])

    def wturn(b, h):
        k = chip(3 if h == 0 else 1, b)
        wwait(k, h)
        wput(k, chip(2, b), zp if h == 0 else zm, h)

    def xput(p, frm, to, target, h=None):
        if h is None:
            put(xg.at[p, frm], xg.at[p, to], xs_sem, xr_sem.at[p, to, 0], target)
        else:
            rows = pl.ds(h * (HALF // 2), HALF // 2)
            put(xg.at[p, frm, rows], xg.at[p, to, rows], xs_sem, xr_sem.at[p, to, h], target)

    def xwait(p, q):
        if RING[q][0] == 2:
            for h in (0, 1):
                rows = pl.ds(h * (HALF // 2), HALF // 2)
                wait_in(xg.at[p, 2 * q, rows], xr_sem.at[p, 2 * q, h])
        else:
            wait_in(xg.at[p, 2 * q], xr_sem.at[p, 2 * q, 0])

    def xfwd(p, q):
        a, b = RING[q]
        xwait(p, q)
        if a == 0:
            xput(p, 2 * q, 2 * chip(3, b), xp)
            xput(p, 2 * q, 2 * chip(1, b), xm)
        elif a == 3:
            xput(p, 2 * q, 2 * chip(2, b), xp, 0)
        elif a == 1:
            xput(p, 2 * q, 2 * chip(2, b), xm, 1)
        xput(p, 2 * q, 2 * q + 1, sib)

    def xsib(p, qs):
        for q in qs:
            wait_in(xg.at[p, 2 * q + 1], xr_sem.at[p, 2 * q + 1, 0])

    def xown(p):
        xput(p, 0, 2 * chip(3, 0), xp)
        xput(p, 0, 2 * chip(1, 0), xm)
        xput(p, 0, 2 * chip(0, 1), yp)

    def lanes_of(p, k):
        return pl.ds(p * 2048 + k * HALF, HALF)

    def bput(buf, p, frm, to, s_sem, r_sem, target):
        put(buf.at[:, lanes_of(p, frm)], buf.at[:, lanes_of(p, to)], s_sem, r_sem.at[p, to], target)

    def bwait(buf, p, k, r_sem):
        wait_in(buf.at[:, lanes_of(p, k)], r_sem.at[p, k])

    def spread0(buf, p, s_sem, r_sem):
        bput(buf, p, 0, 2 * chip(0, 1), s_sem, r_sem, yp)
        bput(buf, p, 0, 2 * chip(2, 0), s_sem, r_sem, x2)
        bput(buf, p, 0, 2 * chip(3, 0), s_sem, r_sem, xp)
        bput(buf, p, 0, 2 * chip(1, 0), s_sem, r_sem, xm)
        bput(buf, p, 0, 1, s_sem, r_sem, sib)

    def spread1(buf, p, s_sem, r_sem):
        k = 2 * chip(0, 1)
        bwait(buf, p, k, r_sem)
        bput(buf, p, k, 2 * chip(2, 1), s_sem, r_sem, x2)
        bput(buf, p, k, 2 * chip(3, 1), s_sem, r_sem, xp)
        bput(buf, p, k, 2 * chip(1, 1), s_sem, r_sem, xm)
        bput(buf, p, k, k + 1, s_sem, r_sem, sib)

    def spread2(buf, p, b, s_sem, r_sem):
        for a in (3, 1, 2):
            k = 2 * chip(a, b)
            bwait(buf, p, k, r_sem)
            bput(buf, p, k, k + 1, s_sem, r_sem, sib)

    def spread3(buf, p, r_sem):
        for q in range(8):
            bwait(buf, p, 2 * q + 1, r_sem)

    RES = (rs_sem, rr_sem)
    CUR = (cs_sem, cr_sem)

    feats = (fa, fb)

    def block(p, q, j0, j1):
        rows = pl.ds(pl.multiple_of(q * 256, 256), 256)
        v = xg[p, pl.ds(2 * q, 2)].reshape(256, KX)
        for j in range(j0, j1):
            u = jnp.dot(v, wg[j], preferred_element_type=F32)
            feats[p][rows, j * 256:(j + 1) * 256] = cosine(u)

    def blocks(p, q0, q1, j0, j1):
        def step(i, carry):
            block(p, q0 + 2 * i, j0, j1)
            block(p, q0 + 2 * i + 1, j0, j1)
            return carry
        lax.fori_loop(0, (q1 - q0) // 2, step, 0)

    def tdot(p, q, n=2):
        return jnp.dot(feats[p][q * 256:(q + n) * 256, :], dirt[...], preferred_element_type=F32)

    def tput(p, q, t, n=2):
        tt = t.T
        for i in range(n):
            tkeep[p, q + i] = tt[:, i * 256:i * 256 + HALF]
            tss[p, q + i] = tt[:, i * 256 + HALF:i * 256 + 256].astype(BF)
            put(tss.at[p, q + i], tsr.at[p, q + i], bs_sem, br_sem.at[p, q + i], sib)

    def tsum(p, q):
        wait_in(tsr.at[p, q], br_sem.at[p, q])
        c = tkeep[p, q] + tsr[p, q].astype(F32)
        if q == 0:
            tkeep[p, 0] = c
        else:
            a, b = RING[q]
            to = chip(-a, b)
            tse[p, q] = c.astype(BF)
            put(tse.at[p, q], trecv.at[p, to], ts_sem, tr_sem.at[p, to], dev(dx=a, dyl=b))

    def curvature(p):
        total = tkeep[p, 0]
        for k in range(1, 8):
            wait_in(trecv.at[p, k], tr_sem.at[p, k])
            total = total + trecv[p, k].astype(F32)
        total = total[0:147]
        pr = prob_ref[:, p * HALF:(p + 1) * HALF].astype(F32)
        mixed = jnp.sum(pr * total, axis=0, keepdims=True)
        curv[0:147, p * 2048:p * 2048 + HALF] = (pr * (total - mixed)).astype(BF)
        spread0(curv, p, *CUR)

    wput(0, chip(3, 0), zp, 0)
    wput(0, chip(1, 0), zm, 1)
    wput(0, chip(0, 1), yq, 0)
    xown(0)
    wput(0, chip(3, 0), zp, 1)
    wput(0, chip(1, 0), zm, 0)
    wput(0, chip(0, 1), yq, 1)
    xput(0, 0, 1, sib)
    xput(1, 0, 1, sib)

    def dput(frm, to, target):
        put(dirg.at[frm], dirg.at[to], ds_sem, dr_sem.at[to], target)

    dput(0, chip(0, 1), yq)

    wturn(0, 0)
    wturn(0, 1)
    xfwd(0, chip(3, 0))
    xfwd(0, chip(1, 0))
    xfwd(0, chip(0, 1))
    xown(1)
    wwait(chip(3, 0), 1)
    wwait(chip(1, 0), 0)
    for h in (0, 1):
        k = chip(0, 1)
        wwait(k, h)
        wput(k, chip(3, 1), zp, h)
        wput(k, chip(1, 1), zm, h)
    xfwd(0, chip(2, 0))
    wwait(chip(2, 0), 0)
    wwait(chip(2, 0), 1)
    xsib(0, range(0, 4))
    blocks(0, 0, 4, 0, 4)

    wturn(1, 0)
    xfwd(0, chip(3, 1))
    xfwd(0, chip(1, 1))
    wturn(1, 1)

    wait_in(dirg.at[chip(0, 1)], dr_sem.at[chip(0, 1)])
    for r in (0, 1):
        k = chip(0, r)
        dput(k, chip(2, r), z2)
        dput(k, chip(3, r), zp)
        dput(k, chip(1, r), zm)
    xfwd(1, chip(3, 0))
    xfwd(1, chip(1, 0))
    xfwd(1, chip(0, 1))
    xfwd(0, chip(2, 1))
    xsib(0, range(4, 8))
    blocks(0, 4, 8, 0, 4)

    xfwd(1, chip(2, 0))
    xfwd(1, chip(3, 1))
    xfwd(1, chip(1, 1))
    spread0(resid, 0, *RES)
    spread0(resid, 1, *RES)
    xsib(1, range(0, 4))
    blocks(1, 0, 4, 0, 4)
    wwait(chip(3, 1), 1)
    wwait(chip(1, 1), 0)
    wwait(chip(2, 1), 0)
    wwait(chip(2, 1), 1)
    blocks(0, 0, 8, 4, 8)
    xfwd(1, chip(2, 1))
    blocks(1, 0, 4, 4, 8)
    spread1(resid, 0, *RES)
    spread1(resid, 1, *RES)
    for r in (0, 1):
        for a in (3, 1, 2):
            wait_in(dirg.at[chip(a, r)], dr_sem.at[chip(a, r)])
    for j in range(8):
        dirt[j * 256:(j + 1) * 256, :] = dirg[j].astype(F32).T.astype(BF)
    xsib(1, range(4, 8))

    for i in range(4):
        t = tdot(0, 2 * i)
        block(1, 4 + i, 0, 8)
        tput(0, 2 * i, t)
        if i:
            tsum(0, 2 * i - 2)
            tsum(0, 2 * i - 1)
    tput(1, 0, tdot(1, 0, 4), 4)
    tsum(0, 6)
    tsum(0, 7)
    tput(1, 4, tdot(1, 4, 4), 4)
    for q in range(4):
        tsum(1, q)
    curvature(0)
    for q in range(4, 8):
        tsum(1, q)
    for p in (0, 1):
        for b in (0, 1):
            spread2(resid, p, b, *RES)
    for p in (0, 1):
        spread3(resid, p, RES[1])

    def share(v, j, own, send, recv, s_sem, r_sem):
        if j == 0:
            own[...] = v[0:147]
        else:
            a, b = RING[j]
            to = chip(-a, b)
            send[j] = v.astype(BF)
            put(send.at[j], recv.at[to], s_sem, r_sem.at[to], dev(dz=a, dyh=b))

    def cols(j):
        return slice(j * 256, (j + 1) * 256)

    order = (7, 5, 6, 4, 3, 1, 2, 0)
    for i, j in enumerate(order):
        v = jnp.dot(resid[:, 0:2048], fa[:, cols(j)], preferred_element_type=F32)
        v = v + jnp.dot(resid[:, 2048:4096], fb[:, cols(j)], preferred_element_type=F32)
        a, b = RING[j]
        if j == 0:
            grad_ref[...] = v[0:147]
        elif a == 0:
            gkeep[...] = v
        else:
            gsend[j] = v.astype(BF)
            to = chip(-a, b)
            put(gsend.at[j], grecv.at[to], gs_sem, gr_sem.at[to], dev(dz=a))
        if i == 2:
            curvature(1)
            spread1(curv, 0, *CUR)
        if i == 5:
            spread2(curv, 0, 0, *CUR)
        if i == 7:
            spread1(curv, 1, *CUR)
    spread2(curv, 0, 1, *CUR)
    spread3(curv, 0, CUR[1])
    for i, j in enumerate(order):
        hacc[:, cols(j)] = jnp.dot(curv[:, 0:2048], fa[:, cols(j)], preferred_element_type=F32)
        if i == 3:
            spread2(curv, 1, 0, *CUR)
    spread2(curv, 1, 1, *CUR)
    far = gkeep[...]
    for a in (3, 1, 2):
        k = chip(a, 1)
        wait_in(grecv.at[k], gr_sem.at[k])
        far = far + grecv[k].astype(F32)
    k = chip(0, 1)
    gsend[k] = far.astype(BF)
    put(gsend.at[k], grecv.at[k], gs_sem, gr_sem.at[k], yq)
    spread3(curv, 1, CUR[1])
    for j in order:
        v = hacc[:, cols(j)] + jnp.dot(curv[:, 2048:4096], fb[:, cols(j)], preferred_element_type=F32)
        share(v, j, hess_ref, hsend, hrecv, hs_sem, hr_sem)

    g = grad_ref[...]
    for k in (chip(3, 0), chip(1, 0), chip(2, 0), chip(0, 1)):
        wait_in(grecv.at[k], gr_sem.at[k])
        g = g + grecv[k].astype(F32)[0:147]
    grad_ref[...] = g
    h = hess_ref[...] + damp_ref[0] * dir_ref[...].astype(F32)
    for k in range(1, 8):
        wait_in(hrecv.at[k], hr_sem.at[k])
        h = h + hrecv[k].astype(F32)[0:147]
    hess_ref[...] = h

    for c in sends:
        c.wait_send()


def on_device(inputs, probs, labels, proj_weight, phase, direction, damping):
    vmem = pl.BlockSpec(memory_space=pltpu.VMEM)
    dma = pltpu.SemaphoreType.DMA
    out = jax.ShapeDtypeStruct(direction.shape, F32)
    return pl.pallas_call(
        kernel,
        out_shape=(out, out),
        in_specs=[vmem] * 6 + [pl.BlockSpec(memory_space=pltpu.SMEM)],
        out_specs=(vmem, vmem),
        scratch_shapes=[
            pltpu.VMEM((2, 16, HALF, KX), BF),
            pltpu.VMEM((8, KX, 256), BF),
            pltpu.VMEM((2048, 2048), BF),
            pltpu.VMEM((2048, 2048), BF),
            pltpu.VMEM((8, CP, 256), BF),
            pltpu.VMEM((2048, CP), BF),
            pltpu.VMEM((2, 8, CP, HALF), F32),
            pltpu.VMEM((2, 8, CP, HALF), BF),
            pltpu.VMEM((2, 8, CP, HALF), BF),
            pltpu.VMEM((2, 8, CP, HALF), BF),
            pltpu.VMEM((2, 8, CP, HALF), BF),
            pltpu.VMEM((CP, 4096), BF),
            pltpu.VMEM((CP, 4096), BF),
            pltpu.VMEM((8, CP, 256), BF),
            pltpu.VMEM((8, CP, 256), BF),
            pltpu.VMEM((8, CP, 256), BF),
            pltpu.VMEM((8, CP, 256), BF),
            pltpu.VMEM((CP, 2048), F32),
            pltpu.VMEM((CP, 256), F32),
            dma((40,)), dma((2, 16, 2)), dma((20,)), dma((8, 2)), dma((8,)), dma((8,)),
            dma((16,)), dma((2, 8)), dma((16,)), dma((2, 8)),
            dma((32,)), dma((2, 16)), dma((32,)), dma((2, 16)),
            dma((8,)), dma((8,)), dma((8,)), dma((8,)),
        ],
        compiler_params=pltpu.CompilerParams(
            collective_id=0, has_side_effects=True, vmem_limit_bytes=56 * 1024 * 1024),
    )(inputs, probs, labels.reshape(1, -1), proj_weight, phase, direction, damping)


def solution(mesh):
    placed = (
        P(None, ("samp", "feat")),
        P(None, ("samp", "feat")),
        P(("samp", "feat")),
        P(None, ("feat", "samp")),
        P(None, ("feat", "samp")),
        P(None, ("feat", "samp")),
        P(),
    )
    return jax.shard_map(
        on_device,
        mesh=mesh,
        in_specs=placed,
        out_specs=(P(None, ("feat", "samp")), P(None, ("feat", "samp"))),
        check_vma=False,
    )
```
